768 devices in a mesh: dp: 64 (over z_lo, y, core), section: 12 (over x, z_hi).
Axes of the slice: x: 4, y: 8, z: 12 (z_hi: 3, z_lo: 4; z = z_hi * 4 + z_lo), core: 2. Of those that a mesh axis runs over, the one named last changes fastest.
Arguments:
- saved_inputs: bfloat16 [12, 64, 2, 384, 2048], P('section', 'dp'), may hold values from -16 to 16
- hidden_grads: bfloat16 [12, 64, 2, 384, 256], P('section', 'dp'), may hold values from -0.029907227 to 0.029907227
- block_expert: int32 [12, 64, 2, 3], P('section', 'dp'), may hold values from 0 to 1, as said below
- live_counts: int32 [12, 64, 2, 2], P('section', 'dp'), may hold values from 0 to 384, as said below
- first_moment: float32 [12, 2048, 2, 256], P('section', 'dp'), may hold values from -3 to 3
- second_moment: float32 [12, 2048, 2, 256], P('section', 'dp'), may hold values from 0.05 to 2
Outputs:
- grad_total: float32 [12, 2048, 2, 256], P('section', 'dp')
- new_first: float32 [12, 2048, 2, 256], P('section', 'dp')
- new_second: float32 [12, 2048, 2, 256], P('section', 'dp')
- step_direction: float32 [12, 2048, 2, 256], P('section', 'dp')
The draws below stay inside these ranges and needn't reach their ends.
Inputs may be any that keep to these rules, and one draw needn't show every extreme that they name: block_expert[p, d, k, b] names the expert of rows b * 128 to (b + 1) * 128 - 1 of that device's direction-k rows. live_counts[p, d, k, e] is 0 when no block of that direction names expert e; for n such blocks it lies between 128 * (n - 1) + 1 and 128 * n. On every device one of the two directions has all its blocks on one expert with all 384 rows live.
All inputs are finite; a program needn't handle non-finite values.
Results may differ from the reference program's by a relative error of at most 0.0021.
Values may be sent and summed in bfloat16 or wider, within the bound.
A program may use at most 64 MiB of HBM per device.

```python
import math
import jax
import jax.numpy as jnp
from jax import lax

D = 2048
FF = 256
EXPERTS = 2
BLOCK = 128
ROWS = 384
NBLK = 3
SECTIONS = 12
RANKS = 64


def routing(key):
    lead_shape = (SECTIONS, RANKS, 2)
    block_draw = jax.random.randint(jax.random.fold_in(key, 101), lead_shape + (NBLK,), 0, EXPERTS)
    full_side = jax.random.randint(jax.random.fold_in(key, 102), (SECTIONS, RANKS, 1), 0, 2)
    full_expert = jax.random.randint(jax.random.fold_in(key, 103), (SECTIONS, RANKS, 1, 1), 0, EXPERTS)
    is_full = jnp.arange(2, dtype=jnp.int32)[None, None, :] == full_side
    block_expert = jnp.where(is_full[..., None], full_expert, block_draw).astype(jnp.int32)
    padding = jax.random.randint(jax.random.fold_in(key, 104), lead_shape + (EXPERTS,), 0, BLOCK)
    padding = jnp.where(is_full[..., None], 0, padding)
    onehot = (block_expert[..., :, None] == jnp.arange(EXPERTS, dtype=jnp.int32)).astype(jnp.int32)
    numbers = jnp.sum(onehot, axis=-2)
    live_counts = jnp.where(numbers > 0, BLOCK * numbers - padding, 0).astype(jnp.int32)
    return (block_expert, live_counts)


def draw_block_expert(key, part):
    return routing(key)[0]


def draw_live_counts(key, part):
    return routing(key)[1]


def raised(array, rng, source, target, shards_of, factor):
    owner, partner = [(jnp.arange(array.shape[axis_at]) // (array.shape[axis_at] // shards_of)).reshape([-1 if axis == axis_at else 1 for axis in range(array.ndim)]) for axis_at in (source, target)]
    chosen = jax.random.permutation(rng, shards_of)[partner]
    strong = (owner == chosen) | (owner == (partner + shards_of // 2) % shards_of)
    return jnp.where(strong, factor * array, array)


def level_of(stream_key, dims, pieces, smallest, largest):
    gain, own = 1.0, jax.random.fold_in(stream_key, 6)
    for axis_at, shards_of in pieces:
        steps = jnp.exp(jax.random.uniform(jax.random.fold_in(own, axis_at), (shards_of,), jnp.float32, smallest / len(pieces), largest / len(pieces)))
        gain = gain * jnp.repeat(steps, dims[axis_at] // shards_of).reshape([-1 if axis == axis_at else 1 for axis in range(len(dims))])
    return gain


def centred(stream_key, dims, width, reach, pieces=(), kind=jnp.bfloat16):
    array = jax.random.normal(stream_key, dims, jnp.float32) * width
    if len(pieces) > 0:
        array = level_of(stream_key, dims, pieces, -0.22, 0.18) * array
    return jnp.clip(array, min=-reach, max=reach).astype(kind)


def heavy_noise(rng, shape, width, reach, cuts, heavy, kind=jnp.bfloat16):
    result = width * jax.random.normal(rng, shape, jnp.float32)
    if cuts:
        result = result * level_of(rng, shape, cuts, -0.22, 0.18)
    return jnp.clip(raised(result, jax.random.fold_in(rng, 3), *heavy), -reach, reach).astype(kind)


def setup_inputs(seed: int = 0) -> dict:
    key_list = jax.random.split(jax.random.key(seed), 7)
    return {
        "saved_inputs": heavy_noise(key_list[0], (SECTIONS, RANKS, 2, ROWS, D), 1.0, 16.0, ((0, 12), (1, 64)), (1, 4, 64, 4.0)),
        "hidden_grads": centred(key_list[1], (SECTIONS, RANKS, 2, ROWS, FF), 0.005, 0.029907227, ((0, 12), (1, 64))),
        "block_expert": draw_block_expert(jax.random.fold_in(key_list[6], 71), 0),
        "live_counts": draw_live_counts(jax.random.fold_in(key_list[6], 71), 0),
        "first_moment": centred(key_list[4], (SECTIONS, D, EXPERTS, FF), 0.5, 3.0, ((0, 12), (1, 64)), jnp.float32),
        "second_moment": jnp.clip(jnp.exp(math.log(2.0) - 3.6888794 * jax.random.uniform(key_list[5], (SECTIONS, D, EXPERTS, FF), jnp.float32) ** level_of(key_list[5], (SECTIONS, D, EXPERTS, FF), ((0, 12), (1, 64)), -0.2, 0.2)), 0.05, 2.0),
    }


beta_one = 0.9
beta_two = 0.95
adam_epsilon = 1e-08
bias_first = 1.0 - 0.9 ** 50
bias_second = 1.0 - 0.95 ** 50

def route_select(block_expert, live_counts):
    experts = jnp.arange(EXPERTS, dtype=jnp.int32)
    onehot = (block_expert[..., :, None] == experts).astype(jnp.int32)
    earlier = jnp.cumsum(onehot, axis=-2) - onehot
    before = lax.optimization_barrier(jnp.sum(earlier * onehot, axis=-1))
    limits = lax.optimization_barrier(jnp.sum(live_counts[..., None, :] * onehot, axis=-1))
    offsets = jnp.arange(BLOCK, dtype=jnp.int32)
    positions = before[..., None] * BLOCK + offsets
    live_rows = positions < limits[..., None]
    return (live_rows, onehot)

def reference(saved_inputs, hidden_grads, block_expert, live_counts, first_moment, second_moment):
    live_rows, onehot = route_select(block_expert, live_counts)
    weights = onehot.astype(jnp.float32)
    masked = hidden_grads.reshape(SECTIONS, RANKS, 2, NBLK, BLOCK, FF).astype(jnp.float32) * live_rows[..., None].astype(jnp.float32)
    inputs = saved_inputs.reshape(SECTIONS, RANKS, 2, NBLK, BLOCK, D)

    def accumulate(rank_index, running):
        rows_in = lax.dynamic_index_in_dim(inputs, rank_index, 1, keepdims=False).astype(jnp.float32)
        grads_in = lax.dynamic_index_in_dim(masked, rank_index, 1, keepdims=False)
        weight_in = lax.dynamic_index_in_dim(weights, rank_index, 1, keepdims=False)
        blocks = jnp.einsum('skbrd,skbrf->skbdf', rows_in, grads_in)
        per_section = jnp.einsum('skbdf,skbe->skdef', blocks, weight_in, precision=lax.Precision.HIGHEST)
        own_part = per_section[:, 0]
        sent_part = lax.optimization_barrier(per_section[:, 1].astype(jnp.bfloat16)).astype(jnp.float32)
        mirror = jnp.roll(sent_part, SECTIONS // 2, axis=0)
        return running + own_part + mirror
    start_sum = jnp.zeros((SECTIONS, D, EXPERTS, FF), jnp.float32)
    grad_total = lax.fori_loop(0, RANKS, accumulate, start_sum)
    new_first = beta_one * first_moment + (1.0 - beta_one) * grad_total
    new_second = beta_two * second_moment + (1.0 - beta_two) * grad_total * grad_total
    step_direction = new_first / bias_first / (jnp.sqrt(new_second / bias_second) + adam_epsilon)
    return (grad_total, new_first, new_second, step_direction)
```

```python
import functools

import jax
import jax.numpy as jnp
from jax import lax
from jax.experimental import pallas as pl
from jax.experimental.pallas import tpu as pltpu
from jax.sharding import PartitionSpec as P

MESH = pl.DeviceIdType.MESH
EXPERTS = 2
BLOCK = 128
NBLK = 3
ROWS = BLOCK * NBLK
D = 2048
FF = 256
WIDE = EXPERTS * FF
HALF = D // 2
YS = 8
ZS = 4

beta_one = 0.9
beta_two = 0.95
adam_epsilon = 1e-08
bias_first = 1.0 - 0.9**50
bias_second = 1.0 - 0.95**50


def kernel(
    be_ref, lc_ref, x_hbm, g_hbm, low_ref, high_ref,
    xb, graw, gb, total, mirror_out, mirror_in, ring_a, ring_b, last, zbuf,
    load_sem, pair_send, pair_recv, mir_send, mir_recv,
    a_send, a_recv, b_send, b_recv, z_send, z_recv,
):
    dp = lax.axis_index("dp")
    sec = lax.axis_index("section")
    core = dp % 2
    y = (dp // 2) % YS
    z = dp // (2 * YS)
    sgn = 1 - 2 * core

    def at(zz, yy, cc):
        return {"dp": zz * (2 * YS) + yy * 2 + cc, "section": sec}

    partner = at(z, y, 1 - core)
    mirror = {"dp": dp, "section": (sec + 6) % 12}
    next_a = at(z, (y + sgn + YS) % YS, core)
    next_b = at(z, (y - sgn + YS) % YS, core)

    def remote(src, dst, send, recv, device):
        return pltpu.make_async_remote_copy(
            src_ref=src, dst_ref=dst, send_sem=send, recv_sem=recv, device_id=device, device_id_type=MESH
        )

    mine = pl.ds(pl.multiple_of(core * HALF, HALF), HALF)
    other = pl.ds(pl.multiple_of((1 - core) * HALF, HALF), HALF)
    load_g = pltpu.make_async_copy(g_hbm, graw, load_sem.at[2])
    load_g.start()
    loads = [pltpu.make_async_copy(x_hbm.at[k, :, mine], xb.at[0, k], load_sem.at[k]) for k in range(2)]
    loads[1].start()
    loads[0].start()

    barrier = pltpu.get_barrier_semaphore()
    peers = [partner, mirror, next_a, next_b]
    for dz in range(1, ZS):
        for cc in range(2):
            peers.append(at((z + dz) % ZS, y, cc))
    for peer in peers:
        pl.semaphore_signal(barrier, inc=1, device_id=peer, device_id_type=MESH)

    load_g.wait()
    rows = lax.broadcasted_iota(jnp.int32, (BLOCK, FF), 0)

    def mask_direction(k):
        for b in range(NBLK):
            owner = be_ref[k, b]
            before = jnp.int32(0)
            for c in range(b):
                before = before + jnp.where(be_ref[k, c] == owner, BLOCK, 0)
            block = graw[k, pl.ds(b * BLOCK, BLOCK), :].astype(jnp.float32)
            for e in range(EXPERTS):
                limit = jnp.where(owner == e, lc_ref[k, e], 0) - before
                kept = jnp.where(rows < limit, block, 0.0).astype(jnp.bfloat16)
                gb[0, k, pl.ds(b * BLOCK, BLOCK), pl.ds(e * FF, FF)] = kept

    mask_direction(1)
    mask_direction(0)
    pl.semaphore_wait(barrier, len(peers))

    send_x = [remote(x_hbm.at[k, :, other], xb.at[1, k], pair_send.at[k], pair_recv.at[k], partner) for k in range(2)]
    send_g = [remote(gb.at[0, k], gb.at[1, k], pair_send.at[2 + k], pair_recv.at[2 + k], partner) for k in range(2)]
    for k in (1, 0):
        send_g[k].start()
        send_x[k].start()

    def off(d):
        return (y + sgn * d + YS) % YS

    first_pair = off(4) // 2

    def tile(k, t, pair):
        columns = pl.ds(pl.multiple_of(t * (HALF // 2) + pair * 128, 128), 128)
        acc = None
        for who in range(2):
            part = lax.dot_general(
                xb[who, k, :, columns],
                gb[who, k],
                (((0,), (0,)), ((), ())),
                preferred_element_type=jnp.float32,
            )
            acc = part if acc is None else acc + part
        return acc

    def mirror_tiles(order):
        n = len(order)

        def body(i, carry):
            t = i % 2
            step = i // 2
            shift = order[0] if n == 1 else jnp.where(step == 0, order[0], order[1])
            pair = (first_pair + shift) % 4
            value = tile(1, t, pair).astype(jnp.bfloat16)
            mirror_out[2 * pair, t] = value[:64]
            mirror_out[2 * pair + 1, t] = value[64:]
            return carry

        lax.fori_loop(0, 2 * n, body, 0)

    def send_mirror(d, slot):
        v = off(d)
        copy = remote(mirror_out.at[v], mirror_in.at[v], mir_send.at[slot], mir_recv.at[slot], mirror)
        copy.start()
        return copy

    loads[1].wait()
    send_g[1].wait_recv()
    send_x[1].wait_recv()
    mirrors = {}
    mirror_tiles([0])
    mirrors[4] = send_mirror(4, 0)
    mirror_tiles([1, 3])
    for slot, d in enumerate((3, -3, 2, -2)):
        mirrors[d] = send_mirror(d, 1 + slot)
    mirror_tiles([2])
    for slot, d in enumerate((1, -1, 0)):
        mirrors[d] = send_mirror(d, 5 + slot)

    loads[0].wait()
    send_g[0].wait_recv()
    send_x[0].wait_recv()

    def own_body(i, carry):
        t = i % 2
        pair = (first_pair + i // 2) % 4
        value = tile(0, t, pair)
        total[2 * pair, t] = value[:64]
        total[2 * pair + 1, t] = value[64:]
        return carry

    lax.fori_loop(0, 8, own_body, 0)

    def add_mirror(d):
        v = off(d)
        mirrors[d].wait_recv()
        total[v] = total[v] + mirror_in[v].astype(jnp.float32)

    sends = []

    def start(src, dst, send, recv, device):
        copy = remote(src, dst, send, recv, device)
        copy.start()
        sends.append(copy)

    def got(ring, sems, ssems, step, t, device):
        remote(ring.at[step, t], ring.at[step, t], ssems.at[step, t], sems.at[step, t], device).wait_recv()

    def forward_a(step, d):
        for t in range(2):
            got(ring_a, a_recv, a_send, step, t, next_a)
            ring_a[step, t] = ring_a[step, t] + total[off(d), t]
            start(ring_a.at[step, t], ring_a.at[step + 1, t], a_send.at[step + 1, t], a_recv.at[step + 1, t], next_a)

    def forward_b(step, d):
        for t in range(2):
            got(ring_b, b_recv, b_send, step, t, next_b)
            ring_b[step, t] = ring_b[step, t] + total[off(d), t]
            start(ring_b.at[step, t], ring_b.at[step + 1, t], b_send.at[step + 1, t], b_recv.at[step + 1, t], next_b)

    add_mirror(4)
    for t in range(2):
        start(total.at[off(4), t], ring_a.at[0, t], a_send.at[0, t], a_recv.at[0, t], next_a)
    add_mirror(3)
    forward_a(0, 3)
    add_mirror(-3)
    for t in range(2):
        start(total.at[off(-3), t], ring_b.at[0, t], b_send.at[0, t], b_recv.at[0, t], next_b)
    add_mirror(2)
    forward_a(1, 2)
    add_mirror(-2)
    forward_b(0, -2)
    add_mirror(1)
    forward_a(2, 1)
    add_mirror(-1)
    forward_b(1, -1)
    add_mirror(0)

    def z_copy(t, k):
        zt = 2 * core + t
        return remote(
            last.at[t, pl.ds(32 * k, 32)], zbuf.at[z], z_send.at[t, k], z_recv.at[z], at(zt, y, k)
        )

    def is_self(t, k):
        return jnp.logical_and(2 * core + t == z, core == k)

    for t in range(2):
        got(ring_a, a_recv, a_send, 3, t, next_a)
        got(ring_b, b_recv, b_send, 2, t, next_b)
        last[t] = total[y, t] + (ring_a[3, t] + ring_b[2, t])
        for k in range(2):

            @pl.when(jnp.logical_not(is_self(t, k)))
            def _():
                z_copy(t, k).start()

            @pl.when(is_self(t, k))
            def _():
                zbuf[z] = last[t, pl.ds(32 * k, 32)]

    def z_wait(source):
        remote(zbuf.at[source], zbuf.at[source], z_send.at[0, 0], z_recv.at[source], partner).wait_recv()

    for dz in range(1, ZS):
        z_wait((z + dz) % ZS)

    @pl.when(core != z // 2)
    def _():
        z_wait(z)

    for i, out_ref in enumerate((low_ref, high_ref)):
        result = zbuf[2 * i] + zbuf[2 * i + 1]
        for e in range(EXPERTS):
            out_ref[:, e, :] = result[:, e * FF : (e + 1) * FF]

    for k in range(2):
        send_x[k].wait_send()
        send_g[k].wait_send()
    for copy in mirrors.values():
        copy.wait_send()
    for copy in sends:
        copy.wait_send()
    for t in range(2):
        for k in range(2):

            @pl.when(jnp.logical_not(is_self(t, k)))
            def _():
                z_copy(t, k).wait_send()


def per_device(saved_inputs, hidden_grads, block_expert, live_counts, first_moment, second_moment):
    any_spec = pl.BlockSpec(memory_space=pl.ANY)
    smem_spec = pl.BlockSpec(memory_space=pltpu.SMEM)
    low, high = pl.pallas_call(
        kernel,
        out_shape=[jax.ShapeDtypeStruct((32, EXPERTS, FF), jnp.float32)] * 2,
        in_specs=[smem_spec, smem_spec, any_spec, any_spec],
        out_specs=[pl.BlockSpec(memory_space=pltpu.VMEM)] * 2,
        scratch_shapes=[
            pltpu.VMEM((2, 2, ROWS, HALF), jnp.bfloat16),
            pltpu.VMEM((2, ROWS, FF), jnp.bfloat16),
            pltpu.VMEM((2, 2, ROWS, WIDE), jnp.bfloat16),
            pltpu.VMEM((YS, 2, 64, WIDE), jnp.float32),
            pltpu.VMEM((YS, 2, 64, WIDE), jnp.bfloat16),
            pltpu.VMEM((YS, 2, 64, WIDE), jnp.bfloat16),
            pltpu.VMEM((4, 2, 64, WIDE), jnp.float32),
            pltpu.VMEM((3, 2, 64, WIDE), jnp.float32),
            pltpu.VMEM((2, 64, WIDE), jnp.float32),
            pltpu.VMEM((ZS, 32, WIDE), jnp.float32),
            pltpu.SemaphoreType.DMA((3,)),
            pltpu.SemaphoreType.DMA((4,)),
            pltpu.SemaphoreType.DMA((4,)),
            pltpu.SemaphoreType.DMA((8,)),
            pltpu.SemaphoreType.DMA((8,)),
            pltpu.SemaphoreType.DMA((4, 2)),
            pltpu.SemaphoreType.DMA((4, 2)),
            pltpu.SemaphoreType.DMA((3, 2)),
            pltpu.SemaphoreType.DMA((3, 2)),
            pltpu.SemaphoreType.DMA((2, 2)),
            pltpu.SemaphoreType.DMA((ZS,)),
        ],
        compiler_params=pltpu.CompilerParams(
            collective_id=0, has_side_effects=True, vmem_limit_bytes=66700000
        ),
    )(
        block_expert.reshape(2, NBLK),
        live_counts.reshape(2, EXPERTS),
        saved_inputs.reshape(2, ROWS, D),
        hidden_grads.reshape(2, ROWS, FF),
    )
    grad_total = low + high
    moment_one = first_moment[0]
    moment_two = second_moment[0]
    new_first = beta_one * moment_one + (1.0 - beta_one) * grad_total
    new_second = beta_two * moment_two + (1.0 - beta_two) * grad_total * grad_total
    step_direction = new_first / bias_first / (jnp.sqrt(new_second / bias_second) + adam_epsilon)
    return (grad_total[None], new_first[None], new_second[None], step_direction[None])


def solution(mesh):
    in_specs = (
        P("section", "dp", None, None, None),
        P("section", "dp", None, None, None),
        P("section", "dp", None, None),
        P("section", "dp", None, None),
        P("section", "dp", None, None),
        P("section", "dp", None, None),
    )
    out_specs = (
        P("section", "dp", None, None),
        P("section", "dp", None, None),
        P("section", "dp", None, None),
        P("section", "dp", None, None),
    )
    return jax.shard_map(
        per_device, mesh=mesh, in_specs=in_specs, out_specs=out_specs, check_vma=False
    )
```

```python
import functools

import jax
import jax.numpy as jnp
from jax import lax
from jax.experimental import pallas as pl
from jax.experimental.pallas import tpu as pltpu
from jax.sharding import PartitionSpec as P

MESH = pl.DeviceIdType.MESH
EXPERTS = 2
BLOCK = 128
NBLK = 3
ROWS = BLOCK * NBLK
D = 2048
FF = 256
WIDE = EXPERTS * FF
HALF = D // 2
YS = 8
ZS = 4

beta_one = 0.9
beta_two = 0.95
adam_epsilon = 1e-08
bias_first = 1.0 - 0.9**50
bias_second = 1.0 - 0.95**50


def kernel(
    be_ref, lc_ref, x_hbm, g_hbm, low_ref, high_ref,
    xb, graw, gb, total, mirror_out, mirror_in, ring_a, ring_b, last, zbuf,
    load_sem, tile_send, tile_recv, pair_send, pair_recv, mir_send, mir_recv,
    a_send, a_recv, b_send, b_recv, z_send, z_recv,
):
    dp = lax.axis_index("dp")
    sec = lax.axis_index("section")
    core = dp % 2
    y = (dp // 2) % YS
    z = dp // (2 * YS)
    sgn = 1 - 2 * core

    def at(zz, yy, cc):
        return {"dp": zz * (2 * YS) + yy * 2 + cc, "section": sec}

    partner = at(z, y, 1 - core)
    mirror = {"dp": dp, "section": (sec + 6) % 12}
    next_a = at(z, (y + sgn + YS) % YS, core)
    next_b = at(z, (y - sgn + YS) % YS, core)

    def remote(src, dst, send, recv, device):
        return pltpu.make_async_remote_copy(
            src_ref=src, dst_ref=dst, send_sem=send, recv_sem=recv, device_id=device, device_id_type=MESH
        )

    mine = pl.ds(pl.multiple_of(core * HALF, HALF), HALF)
    other = pl.ds(pl.multiple_of((1 - core) * HALF, HALF), HALF)
    load_g = pltpu.make_async_copy(g_hbm, graw, load_sem.at[2])
    load_g.start()
    loads = [pltpu.make_async_copy(x_hbm.at[k, :, mine], xb.at[0, k], load_sem.at[k]) for k in range(2)]
    loads[1].start()
    loads[0].start()

    barrier = pltpu.get_barrier_semaphore()
    peers = [partner, mirror, next_a, next_b]
    for dz in range(1, ZS):
        for cc in range(2):
            peers.append(at((z + dz) % ZS, y, cc))
    for peer in peers:
        pl.semaphore_signal(barrier, inc=1, device_id=peer, device_id_type=MESH)

    def off(d):
        return (y + sgn * d + YS) % YS

    first_pair = off(4) // 2
    shifts = (0, 1, 3, 2)

    def columns_of(pair, t, half):
        return pl.ds(pl.multiple_of(half * HALF + t * (HALF // 2) + pair * 128, 128), 128)

    def tile_copy(i, shift, t):
        pair = (first_pair + shift) % 4
        return remote(
            x_hbm.at[1, :, columns_of(pair, t, 1 - core)],
            xb.at[1, 1, :, columns_of(pair, t, 0)],
            tile_send.at[i],
            tile_recv.at[i],
            partner,
        )

    tiles = [tile_copy(2 * i + t, shift, t) for i, shift in enumerate(shifts) for t in range(2)]
    send_x = remote(x_hbm.at[0, :, other], xb.at[1, 0], pair_send.at[2], pair_recv.at[2], partner)
    send_g = [remote(gb.at[0, k], gb.at[1, k], pair_send.at[k], pair_recv.at[k], partner) for k in range(2)]

    rows = lax.broadcasted_iota(jnp.int32, (BLOCK, FF), 0)

    def mask_direction(k):
        for b in range(NBLK):
            owner = be_ref[k, b]
            before = jnp.int32(0)
            for c in range(b):
                before = before + jnp.where(be_ref[k, c] == owner, BLOCK, 0)
            block = graw[k, pl.ds(b * BLOCK, BLOCK), :].astype(jnp.float32)
            for e in range(EXPERTS):
                limit = jnp.where(owner == e, lc_ref[k, e], 0) - before
                kept = jnp.where(rows < limit, block, 0.0).astype(jnp.bfloat16)
                gb[0, k, pl.ds(b * BLOCK, BLOCK), pl.ds(e * FF, FF)] = kept

    pl.semaphore_wait(barrier, len(peers))
    for copy in tiles[:2]:
        copy.start()
    load_g.wait()
    mask_direction(1)
    send_g[1].start()
    for copy in tiles[2:]:
        copy.start()
    mask_direction(0)
    send_g[0].start()
    send_x.start()

    def tile(k, t, pair):
        columns = pl.ds(pl.multiple_of(t * (HALF // 2) + pair * 128, 128), 128)
        acc = None
        for who in range(2):
            part = lax.dot_general(
                xb[who, k, :, columns],
                gb[who, k],
                (((0,), (0,)), ((), ())),
                preferred_element_type=jnp.float32,
            )
            acc = part if acc is None else acc + part
        return acc

    def mirror_tiles(first, count):
        def body(i, carry):
            t = i % 2
            step = i // 2
            shift = jnp.where(step < 2, step, 5 - step)
            pair = (first_pair + shift) % 4
            arrived = xb.at[1, 1, :, columns_of(pair, t, 0)]
            remote(arrived, arrived, tile_send.at[i], tile_recv.at[i], partner).wait_recv()
            value = tile(1, t, pair).astype(jnp.bfloat16)
            mirror_out[2 * pair, t] = value[:64]
            mirror_out[2 * pair + 1, t] = value[64:]
            return carry

        lax.fori_loop(2 * first, 2 * (first + count), body, 0)

    pieces = [(t, k) for t in range(2) for k in range(2)]
    mirrors = {}

    def rows_of(k):
        return pl.ds(32 * k, 32)

    def send_mirror(d, t, k):
        v = off(d)
        copy = remote(
            mirror_out.at[v, t, rows_of(k)],
            mirror_in.at[v, t, rows_of(k)],
            mir_send.at[d + 3, 2 * t + k],
            mir_recv.at[d + 3, 2 * t + k],
            mirror,
        )
        copy.start()
        mirrors[d, t, k] = copy

    def own_tiles(first, count):
        def body(i, carry):
            t = i % 2
            step = i // 2
            shift = jnp.where(step < 2, step, 5 - step)
            pair = (first_pair + shift) % 4
            value = tile(0, t, pair)
            total[2 * pair, t] = value[:64]
            total[2 * pair + 1, t] = value[64:]
            return carry

        lax.fori_loop(2 * first, 2 * (first + count), body, 0)

    loads[1].wait()
    send_g[1].wait_recv()
    mirror_tiles(0, 1)
    for t, k in pieces:
        send_mirror(4, t, k)
    mirror_tiles(1, 2)
    for t, k in pieces:
        send_mirror(-3, t, k)
    for t, k in pieces:
        send_mirror(3, t, k)
    for t, k in pieces:
        send_mirror(2, t, k)
        send_mirror(-2, t, k)
    loads[0].wait()
    send_g[0].wait_recv()
    send_x.wait_recv()
    own_tiles(0, 3)

    def add_mirror(d, t, k):
        v = off(d)
        mirrors[d, t, k].wait_recv()
        total[v, t, rows_of(k)] = total[v, t, rows_of(k)] + mirror_in[v, t, rows_of(k)].astype(jnp.float32)

    sends = []

    def start(src, dst, send, recv, device):
        copy = remote(src, dst, send, recv, device)
        copy.start()
        sends.append(copy)

    def got(ring, ssems, sems, step, t, k, device):
        here = ring.at[step, t, rows_of(k)]
        remote(here, here, ssems.at[step, 2 * t + k], sems.at[step, 2 * t + k], device).wait_recv()

    def hop(ring, ssems, sems, src, step, t, k, device):
        p = 2 * t + k
        start(src, ring.at[step, t, rows_of(k)], ssems.at[step, p], sems.at[step, p], device)

    def forward(ring, ssems, sems, step, d, t, k, device):
        got(ring, ssems, sems, step, t, k, device)
        ring[step, t, rows_of(k)] = ring[step, t, rows_of(k)] + total[off(d), t, rows_of(k)]
        hop(ring, ssems, sems, ring.at[step, t, rows_of(k)], step + 1, t, k, device)

    ways = ((ring_a, a_send, a_recv), (ring_b, b_send, b_recv))

    def forward_a(step, d, t, k):
        add_mirror(d, t, k)
        forward(*ways[0], step, d, t, k, next_a)

    def forward_b(step, d, t, k):
        add_mirror(d, t, k)
        forward(*ways[1], step, d, t, k, next_b)

    for t, k in pieces:
        add_mirror(4, t, k)
        hop(*ways[0], total.at[off(4), t, rows_of(k)], 0, t, k, next_a)
    mirror_tiles(3, 1)
    for t, k in pieces:
        send_mirror(1, t, k)
        send_mirror(-1, t, k)
    for t, k in pieces:
        send_mirror(0, t, k)
    own_tiles(3, 1)
    for t, k in pieces:
        add_mirror(-3, t, k)
        hop(*ways[1], total.at[off(-3), t, rows_of(k)], 0, t, k, next_b)
    for t, k in pieces:
        forward_a(0, 3, t, k)
    for t, k in pieces:
        forward_a(1, 2, t, k)
        forward_b(0, -2, t, k)
    for t, k in pieces:
        forward_a(2, 1, t, k)
        forward_b(1, -1, t, k)

    def z_copy(t, k):
        zt = 2 * core + t
        return remote(last.at[t, rows_of(k)], zbuf.at[z], z_send.at[t, k], z_recv.at[z], at(zt, y, k))

    def is_self(t, k):
        return jnp.logical_and(2 * core + t == z, core == k)

    for t, k in pieces:
        add_mirror(0, t, k)
        got(ring_a, a_send, a_recv, 3, t, k, next_a)
        got(ring_b, b_send, b_recv, 2, t, k, next_b)
        part = rows_of(k)
        last[t, part] = total[y, t, part] + (ring_a[3, t, part] + ring_b[2, t, part])

        @pl.when(jnp.logical_not(is_self(t, k)))
        def _():
            z_copy(t, k).start()

        @pl.when(is_self(t, k))
        def _():
            zbuf[z] = last[t, part]

    def z_wait(source):
        remote(zbuf.at[source], zbuf.at[source], z_send.at[0, 0], z_recv.at[source], partner).wait_recv()

    for dz in range(1, ZS):
        z_wait((z + dz) % ZS)

    @pl.when(core != z // 2)
    def _():
        z_wait(z)

    for i, out_ref in enumerate((low_ref, high_ref)):
        result = zbuf[2 * i] + zbuf[2 * i + 1]
        for e in range(EXPERTS):
            out_ref[:, e, :] = result[:, e * FF : (e + 1) * FF]

    for copy in (*tiles, send_x, *send_g):
        copy.wait_send()
    for copy in mirrors.values():
        copy.wait_send()
    for copy in sends:
        copy.wait_send()
    for t in range(2):
        for k in range(2):

            @pl.when(jnp.logical_not(is_self(t, k)))
            def _():
                z_copy(t, k).wait_send()


def per_device(saved_inputs, hidden_grads, block_expert, live_counts, first_moment, second_moment):
    any_spec = pl.BlockSpec(memory_space=pl.ANY)
    smem_spec = pl.BlockSpec(memory_space=pltpu.SMEM)
    low, high = pl.pallas_call(
        kernel,
        out_shape=[jax.ShapeDtypeStruct((32, EXPERTS, FF), jnp.float32)] * 2,
        in_specs=[smem_spec, smem_spec, any_spec, any_spec],
        out_specs=[pl.BlockSpec(memory_space=pltpu.VMEM)] * 2,
        scratch_shapes=[
            pltpu.VMEM((2, 2, ROWS, HALF), jnp.bfloat16),
            pltpu.VMEM((2, ROWS, FF), jnp.bfloat16),
            pltpu.VMEM((2, 2, ROWS, WIDE), jnp.bfloat16),
            pltpu.VMEM((YS, 2, 64, WIDE), jnp.float32),
            pltpu.VMEM((YS, 2, 64, WIDE), jnp.bfloat16),
            pltpu.VMEM((YS, 2, 64, WIDE), jnp.bfloat16),
            pltpu.VMEM((4, 2, 64, WIDE), jnp.float32),
            pltpu.VMEM((3, 2, 64, WIDE), jnp.float32),
            pltpu.VMEM((2, 64, WIDE), jnp.float32),
            pltpu.VMEM((ZS, 32, WIDE), jnp.float32),
            pltpu.SemaphoreType.DMA((3,)),
            pltpu.SemaphoreType.DMA((8,)),
            pltpu.SemaphoreType.DMA((8,)),
            pltpu.SemaphoreType.DMA((3,)),
            pltpu.SemaphoreType.DMA((3,)),
            pltpu.SemaphoreType.DMA((8, 4)),
            pltpu.SemaphoreType.DMA((8, 4)),
            pltpu.SemaphoreType.DMA((4, 4)),
            pltpu.SemaphoreType.DMA((4, 4)),
            pltpu.SemaphoreType.DMA((3, 4)),
            pltpu.SemaphoreType.DMA((3, 4)),
            pltpu.SemaphoreType.DMA((2, 2)),
            pltpu.SemaphoreType.DMA((ZS,)),
        ],
        compiler_params=pltpu.CompilerParams(
            collective_id=0, has_side_effects=True, vmem_limit_bytes=66700000
        ),
    )(
        block_expert.reshape(2, NBLK),
        live_counts.reshape(2, EXPERTS),
        saved_inputs.reshape(2, ROWS, D),
        hidden_grads.reshape(2, ROWS, FF),
    )
    grad_total = low + high
    moment_one = first_moment[0]
    moment_two = second_moment[0]
    new_first = beta_one * moment_one + (1.0 - beta_one) * grad_total
    new_second = beta_two * moment_two + (1.0 - beta_two) * grad_total * grad_total
    step_direction = new_first / bias_first / (jnp.sqrt(new_second / bias_second) + adam_epsilon)
    return (grad_total[None], new_first[None], new_second[None], step_direction[None])


def solution(mesh):
    in_specs = (
        P("section", "dp", None, None, None),
        P("section", "dp", None, None, None),
        P("section", "dp", None, None),
        P("section", "dp", None, None),
        P("section", "dp", None, None),
        P("section", "dp", None, None),
    )
    out_specs = (
        P("section", "dp", None, None),
        P("section", "dp", None, None),
        P("section", "dp", None, None),
        P("section", "dp", None, None),
    )
    return jax.shard_map(
        per_device, mesh=mesh, in_specs=in_specs, out_specs=out_specs, check_vma=False
    )
```

```python
import functools

import jax
import jax.numpy as jnp
from jax import lax
from jax.experimental import pallas as pl
from jax.experimental.pallas import tpu as pltpu
from jax.sharding import PartitionSpec as P

MESH = pl.DeviceIdType.MESH
EXPERTS = 2
BLOCK = 128
NBLK = 3
ROWS = BLOCK * NBLK
D = 2048
FF = 256
WIDE = EXPERTS * FF
HALF = D // 2
YS = 8
ZS = 4

beta_one = 0.9
beta_two = 0.95
adam_epsilon = 1e-08
bias_first = 1.0 - 0.9**50
bias_second = 1.0 - 0.95**50


def kernel(
    be_ref, lc_ref, x_hbm, g_hbm, low_ref, high_ref,
    xb, graw, gb, total, mirror_out, mirror_in, ring_a, ring_b, last, zbuf,
    load_sem, tile_send, tile_recv, pair_send, pair_recv, mir_send, mir_recv,
    a_send, a_recv, b_send, b_recv, z_send, z_recv, word_x, word_up, word_down,
):
    dp = lax.axis_index("dp")
    sec = lax.axis_index("section")
    core = dp % 2
    y = (dp // 2) % YS
    z = dp // (2 * YS)
    sgn = 1 - 2 * core

    def at(zz, yy, cc):
        return {"dp": zz * (2 * YS) + yy * 2 + cc, "section": sec}

    partner = at(z, y, 1 - core)
    mirror = {"dp": dp, "section": (sec + 6) % 12}
    next_a = at(z, (y + sgn + YS) % YS, core)
    next_b = at(z, (y - sgn + YS) % YS, core)

    def remote(src, dst, send, recv, device):
        return pltpu.make_async_remote_copy(
            src_ref=src, dst_ref=dst, send_sem=send, recv_sem=recv, device_id=device, device_id_type=MESH
        )

    mine = pl.ds(pl.multiple_of(core * HALF, HALF), HALF)
    other = pl.ds(pl.multiple_of((1 - core) * HALF, HALF), HALF)
    load_g = pltpu.make_async_copy(g_hbm, graw, load_sem.at[2])
    load_g.start()
    loads = [pltpu.make_async_copy(x_hbm.at[k, :, mine], xb.at[0, k], load_sem.at[k]) for k in range(2)]
    loads[1].start()
    loads[0].start()

    x_up = {"dp": dp, "section": (sec + 3) % 12}
    x_down = {"dp": dp, "section": (sec + 9) % 12}
    z_up = at(z + 1, y, core)
    z_down = at(z - 1, y, core)

    def signal(sem, device):
        pl.semaphore_signal(sem, inc=1, device_id=device, device_id_type=MESH)

    barrier = pltpu.get_barrier_semaphore()
    peers = [partner, next_a, next_b, x_up, x_down]
    for peer in peers:
        signal(barrier, peer)

    @pl.when(z < ZS - 1)
    def _():
        signal(barrier, z_up)

    @pl.when(z > 0)
    def _():
        signal(barrier, z_down)

    n_peers = len(peers) + (z + 2) // 3 + (5 - z) // 3

    def pass_word(step):
        if step > 0:

            @pl.when(z >= step)
            def _():
                pl.semaphore_wait(word_up.at[step - 1], 1)

            @pl.when(z <= ZS - 1 - step)
            def _():
                pl.semaphore_wait(word_down.at[step - 1], 1)

        if step < ZS - 1:

            @pl.when(jnp.logical_and(z >= step, z < ZS - 1))
            def _():
                signal(word_up.at[step], z_up)

            @pl.when(jnp.logical_and(z <= ZS - 1 - step, z > 0))
            def _():
                signal(word_down.at[step], z_down)

    def off(d):
        return (y + sgn * d + YS) % YS

    first_pair = off(4) // 2
    shifts = (0, 1, 3, 2)

    def columns_of(pair, t, half):
        return pl.ds(pl.multiple_of(half * HALF + t * (HALF // 2) + pair * 128, 128), 128)

    def tile_copy(i, shift, t):
        pair = (first_pair + shift) % 4
        return remote(
            x_hbm.at[1, :, columns_of(pair, t, 1 - core)],
            xb.at[1, 1, :, columns_of(pair, t, 0)],
            tile_send.at[i],
            tile_recv.at[i],
            partner,
        )

    tiles = [tile_copy(2 * i + t, shift, t) for i, shift in enumerate(shifts) for t in range(2)]
    send_x = remote(x_hbm.at[0, :, other], xb.at[1, 0], pair_send.at[2], pair_recv.at[2], partner)
    send_g = [remote(gb.at[0, k], gb.at[1, k], pair_send.at[k], pair_recv.at[k], partner) for k in range(2)]

    rows = lax.broadcasted_iota(jnp.int32, (BLOCK, FF), 0)

    def mask_direction(k):
        for b in range(NBLK):
            owner = be_ref[k, b]
            before = jnp.int32(0)
            for c in range(b):
                before = before + jnp.where(be_ref[k, c] == owner, BLOCK, 0)
            block = graw[k, pl.ds(b * BLOCK, BLOCK), :].astype(jnp.float32)
            for e in range(EXPERTS):
                limit = jnp.where(owner == e, lc_ref[k, e], 0) - before
                kept = jnp.where(rows < limit, block, 0.0).astype(jnp.bfloat16)
                gb[0, k, pl.ds(b * BLOCK, BLOCK), pl.ds(e * FF, FF)] = kept

    pl.semaphore_wait(barrier, n_peers)
    for copy in tiles[:2]:
        copy.start()
    signal(word_x, x_up)
    pass_word(0)
    load_g.wait()
    mask_direction(1)
    send_g[1].start()
    for copy in tiles[2:]:
        copy.start()
    mask_direction(0)
    send_g[0].start()
    send_x.start()

    def tile(k, t, pair):
        columns = pl.ds(pl.multiple_of(t * (HALF // 2) + pair * 128, 128), 128)
        acc = None
        for who in range(2):
            part = lax.dot_general(
                xb[who, k, :, columns],
                gb[who, k],
                (((0,), (0,)), ((), ())),
                preferred_element_type=jnp.float32,
            )
            acc = part if acc is None else acc + part
        return acc

    def mirror_tiles(first, count):
        def body(i, carry):
            t = i % 2
            step = i // 2
            shift = jnp.where(step < 2, step, 5 - step)
            pair = (first_pair + shift) % 4
            arrived = xb.at[1, 1, :, columns_of(pair, t, 0)]
            remote(arrived, arrived, tile_send.at[i], tile_recv.at[i], partner).wait_recv()
            value = tile(1, t, pair).astype(jnp.bfloat16)
            mirror_out[2 * pair, t] = value[:64]
            mirror_out[2 * pair + 1, t] = value[64:]
            return carry

        lax.fori_loop(2 * first, 2 * (first + count), body, 0)

    pieces = [(t, k) for t in range(2) for k in range(2)]
    mirrors = {}

    def rows_of(k):
        return pl.ds(32 * k, 32)

    def send_mirror(d, t, k):
        v = off(d)
        copy = remote(
            mirror_out.at[v, t, rows_of(k)],
            mirror_in.at[v, t, rows_of(k)],
            mir_send.at[d + 3, 2 * t + k],
            mir_recv.at[d + 3, 2 * t + k],
            mirror,
        )
        copy.start()
        mirrors[d, t, k] = copy

    def own_tiles(first, count):
        def body(i, carry):
            t = i % 2
            step = i // 2
            shift = jnp.where(step < 2, step, 5 - step)
            pair = (first_pair + shift) % 4
            value = tile(0, t, pair)
            total[2 * pair, t] = value[:64]
            total[2 * pair + 1, t] = value[64:]
            return carry

        lax.fori_loop(2 * first, 2 * (first + count), body, 0)

    loads[1].wait()
    send_g[1].wait_recv()
    mirror_tiles(0, 1)
    pl.semaphore_wait(word_x, 1)
    for t, k in pieces:
        send_mirror(4, t, k)
    mirror_tiles(1, 2)
    for t, k in pieces:
        send_mirror(-3, t, k)
    for t, k in pieces:
        send_mirror(3, t, k)
    for t, k in pieces:
        send_mirror(2, t, k)
        send_mirror(-2, t, k)
    loads[0].wait()
    send_g[0].wait_recv()
    send_x.wait_recv()
    own_tiles(0, 3)

    def add_mirror(d, t, k):
        v = off(d)
        mirrors[d, t, k].wait_recv()
        total[v, t, rows_of(k)] = total[v, t, rows_of(k)] + mirror_in[v, t, rows_of(k)].astype(jnp.float32)

    sends = []

    def start(src, dst, send, recv, device):
        copy = remote(src, dst, send, recv, device)
        copy.start()
        sends.append(copy)

    def got(ring, ssems, sems, step, t, k, device):
        here = ring.at[step, t, rows_of(k)]
        remote(here, here, ssems.at[step, 2 * t + k], sems.at[step, 2 * t + k], device).wait_recv()

    def hop(ring, ssems, sems, src, step, t, k, device):
        p = 2 * t + k
        start(src, ring.at[step, t, rows_of(k)], ssems.at[step, p], sems.at[step, p], device)

    def forward(ring, ssems, sems, step, d, t, k, device):
        got(ring, ssems, sems, step, t, k, device)
        ring[step, t, rows_of(k)] = ring[step, t, rows_of(k)] + total[off(d), t, rows_of(k)]
        hop(ring, ssems, sems, ring.at[step, t, rows_of(k)], step + 1, t, k, device)

    ways = ((ring_a, a_send, a_recv), (ring_b, b_send, b_recv))

    def forward_a(step, d, t, k):
        add_mirror(d, t, k)
        forward(*ways[0], step, d, t, k, next_a)

    def forward_b(step, d, t, k):
        add_mirror(d, t, k)
        forward(*ways[1], step, d, t, k, next_b)

    for t, k in pieces:
        add_mirror(4, t, k)
        hop(*ways[0], total.at[off(4), t, rows_of(k)], 0, t, k, next_a)
    pass_word(1)
    mirror_tiles(3, 1)
    for t, k in pieces:
        send_mirror(1, t, k)
        send_mirror(-1, t, k)
    for t, k in pieces:
        send_mirror(0, t, k)
    own_tiles(3, 1)
    for t, k in pieces:
        add_mirror(-3, t, k)
        hop(*ways[1], total.at[off(-3), t, rows_of(k)], 0, t, k, next_b)
    pass_word(2)
    for t, k in pieces:
        forward_a(0, 3, t, k)
    pass_word(3)
    for t, k in pieces:
        forward_a(1, 2, t, k)
        forward_b(0, -2, t, k)
    for t, k in pieces:
        forward_a(2, 1, t, k)
        forward_b(1, -1, t, k)

    def z_copy(t, k):
        zt = 2 * core + t
        return remote(last.at[t, rows_of(k)], zbuf.at[z], z_send.at[t, k], z_recv.at[z], at(zt, y, k))

    def is_self(t, k):
        return jnp.logical_and(2 * core + t == z, core == k)

    for t, k in pieces:
        add_mirror(0, t, k)
        got(ring_a, a_send, a_recv, 3, t, k, next_a)
        got(ring_b, b_send, b_recv, 2, t, k, next_b)
        part = rows_of(k)
        last[t, part] = total[y, t, part] + (ring_a[3, t, part] + ring_b[2, t, part])

        @pl.when(jnp.logical_not(is_self(t, k)))
        def _():
            z_copy(t, k).start()

        @pl.when(is_self(t, k))
        def _():
            zbuf[z] = last[t, part]

    def z_wait(source):
        remote(zbuf.at[source], zbuf.at[source], z_send.at[0, 0], z_recv.at[source], partner).wait_recv()

    for dz in range(1, ZS):
        z_wait((z + dz) % ZS)

    @pl.when(core != z // 2)
    def _():
        z_wait(z)

    for i, out_ref in enumerate((low_ref, high_ref)):
        result = zbuf[2 * i] + zbuf[2 * i + 1]
        for e in range(EXPERTS):
            out_ref[:, e, :] = result[:, e * FF : (e + 1) * FF]

    for copy in (*tiles, send_x, *send_g):
        copy.wait_send()
    for copy in mirrors.values():
        copy.wait_send()
    for copy in sends:
        copy.wait_send()
    for t in range(2):
        for k in range(2):

            @pl.when(jnp.logical_not(is_self(t, k)))
            def _():
                z_copy(t, k).wait_send()


def per_device(saved_inputs, hidden_grads, block_expert, live_counts, first_moment, second_moment):
    any_spec = pl.BlockSpec(memory_space=pl.ANY)
    smem_spec = pl.BlockSpec(memory_space=pltpu.SMEM)
    low, high = pl.pallas_call(
        kernel,
        out_shape=[jax.ShapeDtypeStruct((32, EXPERTS, FF), jnp.float32)] * 2,
        in_specs=[smem_spec, smem_spec, any_spec, any_spec],
        out_specs=[pl.BlockSpec(memory_space=pltpu.VMEM)] * 2,
        scratch_shapes=[
            pltpu.VMEM((2, 2, ROWS, HALF), jnp.bfloat16),
            pltpu.VMEM((2, ROWS, FF), jnp.bfloat16),
            pltpu.VMEM((2, 2, ROWS, WIDE), jnp.bfloat16),
            pltpu.VMEM((YS, 2, 64, WIDE), jnp.float32),
            pltpu.VMEM((YS, 2, 64, WIDE), jnp.bfloat16),
            pltpu.VMEM((YS, 2, 64, WIDE), jnp.bfloat16),
            pltpu.VMEM((4, 2, 64, WIDE), jnp.float32),
            pltpu.VMEM((3, 2, 64, WIDE), jnp.float32),
            pltpu.VMEM((2, 64, WIDE), jnp.float32),
            pltpu.VMEM((ZS, 32, WIDE), jnp.float32),
            pltpu.SemaphoreType.DMA((3,)),
            pltpu.SemaphoreType.DMA((8,)),
            pltpu.SemaphoreType.DMA((8,)),
            pltpu.SemaphoreType.DMA((3,)),
            pltpu.SemaphoreType.DMA((3,)),
            pltpu.SemaphoreType.DMA((8, 4)),
            pltpu.SemaphoreType.DMA((8, 4)),
            pltpu.SemaphoreType.DMA((4, 4)),
            pltpu.SemaphoreType.DMA((4, 4)),
            pltpu.SemaphoreType.DMA((3, 4)),
            pltpu.SemaphoreType.DMA((3, 4)),
            pltpu.SemaphoreType.DMA((2, 2)),
            pltpu.SemaphoreType.DMA((ZS,)),
            pltpu.SemaphoreType.REGULAR,
            pltpu.SemaphoreType.REGULAR((ZS - 1,)),
            pltpu.SemaphoreType.REGULAR((ZS - 1,)),
        ],
        compiler_params=pltpu.CompilerParams(
            collective_id=0, has_side_effects=True, vmem_limit_bytes=66700000
        ),
    )(
        block_expert.reshape(2, NBLK),
        live_counts.reshape(2, EXPERTS),
        saved_inputs.reshape(2, ROWS, D),
        hidden_grads.reshape(2, ROWS, FF),
    )
    grad_total = low + high
    moment_one = first_moment[0]
    moment_two = second_moment[0]
    new_first = beta_one * moment_one + (1.0 - beta_one) * grad_total
    new_second = beta_two * moment_two + (1.0 - beta_two) * grad_total * grad_total
    step_direction = new_first / bias_first / (jnp.sqrt(new_second / bias_second) + adam_epsilon)
    return (grad_total[None], new_first[None], new_second[None], step_direction[None])


def solution(mesh):
    in_specs = (
        P("section", "dp", None, None, None),
        P("section", "dp", None, None, None),
        P("section", "dp", None, None),
        P("section", "dp", None, None),
        P("section", "dp", None, None),
        P("section", "dp", None, None),
    )
    out_specs = (
        P("section", "dp", None, None),
        P("section", "dp", None, None),
        P("section", "dp", None, None),
        P("section", "dp", None, None),
    )
    return jax.shard_map(
        per_device, mesh=mesh, in_specs=in_specs, out_specs=out_specs, check_vma=False
    )
```

```python
import functools

import jax
import jax.numpy as jnp
from jax import lax
from jax.experimental import pallas as pl
from jax.experimental.pallas import tpu as pltpu
from jax.sharding import PartitionSpec as P

MESH = pl.DeviceIdType.MESH
EXPERTS = 2
BLOCK = 128
NBLK = 3
ROWS = BLOCK * NBLK
D = 2048
FF = 256
WIDE = EXPERTS * FF
HALF = D // 2
YS = 8
ZS = 4

beta_one = 0.9
beta_two = 0.95
adam_epsilon = 1e-08
bias_first = 1.0 - 0.9**50
bias_second = 1.0 - 0.95**50


def kernel(
    be_ref, lc_ref, x_hbm, g_hbm, out_ref,
    xb, graw, gb, total, mirror_out, mirror_in, ring_a, ring_b, last, zbuf,
    load_sem, tile_send, tile_recv, pair_send, pair_recv, mir_send, mir_recv,
    a_send, a_recv, b_send, b_recv, z_send, z_recv, word_x, word_up, word_down,
):
    dp = lax.axis_index("dp")
    sec = lax.axis_index("section")
    core = dp % 2
    y = (dp // 2) % YS
    z = dp // (2 * YS)
    sgn = 1 - 2 * core

    def at(zz, yy, cc):
        return {"dp": zz * (2 * YS) + yy * 2 + cc, "section": sec}

    partner = at(z, y, 1 - core)
    mirror = {"dp": dp, "section": (sec + 6) % 12}
    next_a = at(z, (y + sgn + YS) % YS, core)
    next_b = at(z, (y - sgn + YS) % YS, core)

    def remote(src, dst, send, recv, device):
        return pltpu.make_async_remote_copy(
            src_ref=src, dst_ref=dst, send_sem=send, recv_sem=recv, device_id=device, device_id_type=MESH
        )

    mine = pl.ds(pl.multiple_of(core * HALF, HALF), HALF)
    other = pl.ds(pl.multiple_of((1 - core) * HALF, HALF), HALF)
    load_g = pltpu.make_async_copy(g_hbm, graw, load_sem.at[2])
    load_g.start()
    loads = [pltpu.make_async_copy(x_hbm.at[k, :, mine], xb.at[0, k], load_sem.at[k]) for k in range(2)]
    loads[1].start()
    loads[0].start()

    x_up = {"dp": dp, "section": (sec + 3) % 12}
    x_down = {"dp": dp, "section": (sec + 9) % 12}
    z_up = at(z + 1, y, core)
    z_down = at(z - 1, y, core)

    def signal(sem, device):
        pl.semaphore_signal(sem, inc=1, device_id=device, device_id_type=MESH)

    barrier = pltpu.get_barrier_semaphore()
    peers = [partner, next_a, next_b, x_up, x_down]
    for peer in peers:
        signal(barrier, peer)

    @pl.when(z < ZS - 1)
    def _():
        signal(barrier, z_up)

    @pl.when(z > 0)
    def _():
        signal(barrier, z_down)

    n_peers = len(peers) + (z + 2) // 3 + (5 - z) // 3

    def pass_word(step):
        if step > 0:

            @pl.when(z >= step)
            def _():
                pl.semaphore_wait(word_up.at[step - 1], 1)

            @pl.when(z <= ZS - 1 - step)
            def _():
                pl.semaphore_wait(word_down.at[step - 1], 1)

        if step < ZS - 1:

            @pl.when(jnp.logical_and(z >= step, z < ZS - 1))
            def _():
                signal(word_up.at[step], z_up)

            @pl.when(jnp.logical_and(z <= ZS - 1 - step, z > 0))
            def _():
                signal(word_down.at[step], z_down)

    def off(d):
        return (y + sgn * d + YS) % YS

    first_pair = off(4) // 2
    shifts = (0, 1, 3, 2)

    def columns_of(pair, t, half):
        return pl.ds(pl.multiple_of(half * HALF + t * (HALF // 2) + pair * 128, 128), 128)

    def tile_copy(i, shift, t):
        pair = (first_pair + shift) % 4
        return remote(
            x_hbm.at[1, :, columns_of(pair, t, 1 - core)],
            xb.at[1, 1, :, columns_of(pair, t, 0)],
            tile_send.at[i],
            tile_recv.at[i],
            partner,
        )

    tiles = [tile_copy(2 * i + t, shift, t) for i, shift in enumerate(shifts) for t in range(2)]
    send_x = remote(x_hbm.at[0, :, other], xb.at[1, 0], pair_send.at[2], pair_recv.at[2], partner)
    send_g = [remote(gb.at[0, k], gb.at[1, k], pair_send.at[k], pair_recv.at[k], partner) for k in range(2)]

    rows = lax.broadcasted_iota(jnp.int32, (BLOCK, FF), 0)

    def mask_direction(k):
        for b in range(NBLK):
            owner = be_ref[k, b]
            before = jnp.int32(0)
            for c in range(b):
                before = before + jnp.where(be_ref[k, c] == owner, BLOCK, 0)
            block = graw[k, pl.ds(b * BLOCK, BLOCK), :].astype(jnp.float32)
            for e in range(EXPERTS):
                limit = jnp.where(owner == e, lc_ref[k, e], 0) - before
                kept = jnp.where(rows < limit, block, 0.0).astype(jnp.bfloat16)
                gb[0, k, pl.ds(b * BLOCK, BLOCK), pl.ds(e * FF, FF)] = kept

    pl.semaphore_wait(barrier, n_peers)
    for copy in tiles[:2]:
        copy.start()
    signal(word_x, x_up)
    pass_word(0)
    load_g.wait()
    mask_direction(1)
    send_g[1].start()
    for copy in tiles[2:]:
        copy.start()
    mask_direction(0)
    send_g[0].start()
    send_x.start()

    def tile(k, t, pair):
        columns = pl.ds(pl.multiple_of(t * (HALF // 2) + pair * 128, 128), 128)
        acc = None
        for who in range(2):
            part = lax.dot_general(
                xb[who, k, :, columns],
                gb[who, k],
                (((0,), (0,)), ((), ())),
                preferred_element_type=jnp.float32,
            )
            acc = part if acc is None else acc + part
        return acc

    def mirror_tiles(first, count):
        def body(i, carry):
            t = i % 2
            step = i // 2
            shift = jnp.where(step < 2, step, 5 - step)
            pair = (first_pair + shift) % 4
            arrived = xb.at[1, 1, :, columns_of(pair, t, 0)]
            remote(arrived, arrived, tile_send.at[i], tile_recv.at[i], partner).wait_recv()
            value = tile(1, t, pair).astype(jnp.bfloat16)
            mirror_out[2 * pair, t] = value[:64]
            mirror_out[2 * pair + 1, t] = value[64:]
            return carry

        lax.fori_loop(2 * first, 2 * (first + count), body, 0)

    pieces = [(t, k) for t in range(2) for k in range(2)]
    mirrors = {}

    def rows_of(k):
        return pl.ds(32 * k, 32)

    def send_mirror(d, t, k):
        v = off(d)
        copy = remote(
            mirror_out.at[v, t, rows_of(k)],
            mirror_in.at[v, t, rows_of(k)],
            mir_send.at[d + 3, 2 * t + k],
            mir_recv.at[d + 3, 2 * t + k],
            mirror,
        )
        copy.start()
        mirrors[d, t, k] = copy

    def own_tiles(first, count):
        def body(i, carry):
            t = i % 2
            step = i // 2
            shift = jnp.where(step < 2, step, 5 - step)
            pair = (first_pair + shift) % 4
            value = tile(0, t, pair)
            total[2 * pair, t] = value[:64]
            total[2 * pair + 1, t] = value[64:]
            return carry

        lax.fori_loop(2 * first, 2 * (first + count), body, 0)

    loads[1].wait()
    send_g[1].wait_recv()
    mirror_tiles(0, 1)
    pl.semaphore_wait(word_x, 1)
    for t, k in pieces:
        send_mirror(4, t, k)
    mirror_tiles(1, 2)
    for t, k in pieces:
        send_mirror(-3, t, k)
    for t, k in pieces:
        send_mirror(3, t, k)
    for t, k in pieces:
        send_mirror(2, t, k)
        send_mirror(-2, t, k)
    loads[0].wait()
    send_g[0].wait_recv()
    send_x.wait_recv()
    own_tiles(0, 3)

    def add_mirror(d, t, k):
        v = off(d)
        mirrors[d, t, k].wait_recv()
        total[v, t, rows_of(k)] = total[v, t, rows_of(k)] + mirror_in[v, t, rows_of(k)].astype(jnp.float32)

    sends = []

    def start(src, dst, send, recv, device):
        copy = remote(src, dst, send, recv, device)
        copy.start()
        sends.append(copy)

    def got(ring, ssems, sems, step, t, k, device):
        here = ring.at[step, t, rows_of(k)]
        remote(here, here, ssems.at[step, 2 * t + k], sems.at[step, 2 * t + k], device).wait_recv()

    def hop(ring, ssems, sems, src, step, t, k, device):
        p = 2 * t + k
        start(src, ring.at[step, t, rows_of(k)], ssems.at[step, p], sems.at[step, p], device)

    def forward(ring, ssems, sems, step, d, t, k, device):
        got(ring, ssems, sems, step, t, k, device)
        ring[step, t, rows_of(k)] = ring[step, t, rows_of(k)] + total[off(d), t, rows_of(k)]
        hop(ring, ssems, sems, ring.at[step, t, rows_of(k)], step + 1, t, k, device)

    ways = ((ring_a, a_send, a_recv), (ring_b, b_send, b_recv))

    def forward_a(step, d, t, k):
        add_mirror(d, t, k)
        forward(*ways[0], step, d, t, k, next_a)

    def forward_b(step, d, t, k):
        add_mirror(d, t, k)
        forward(*ways[1], step, d, t, k, next_b)

    for t, k in pieces:
        add_mirror(4, t, k)
        hop(*ways[0], total.at[off(4), t, rows_of(k)], 0, t, k, next_a)
    pass_word(1)
    mirror_tiles(3, 1)
    for t, k in pieces:
        send_mirror(1, t, k)
        send_mirror(-1, t, k)
    for t, k in pieces:
        send_mirror(0, t, k)
    own_tiles(3, 1)
    for t, k in pieces:
        add_mirror(-3, t, k)
        hop(*ways[1], total.at[off(-3), t, rows_of(k)], 0, t, k, next_b)
    pass_word(2)
    for t, k in pieces:
        forward_a(0, 3, t, k)
    pass_word(3)
    for t, k in pieces:
        forward_a(1, 2, t, k)
        forward_b(0, -2, t, k)
    for t, k in pieces:
        forward_a(2, 1, t, k)
        forward_b(1, -1, t, k)

    def z_copy(t, k):
        zt = 2 * core + t
        return remote(last.at[t, rows_of(k)], zbuf.at[z], z_send.at[t, k], z_recv.at[z], at(zt, y, k))

    def is_self(t, k):
        return jnp.logical_and(2 * core + t == z, core == k)

    for t, k in pieces:
        add_mirror(0, t, k)
        got(ring_a, a_send, a_recv, 3, t, k, next_a)
        got(ring_b, b_send, b_recv, 2, t, k, next_b)
        part = rows_of(k)
        last[t, part] = total[y, t, part] + (ring_a[3, t, part] + ring_b[2, t, part])

        @pl.when(jnp.logical_not(is_self(t, k)))
        def _():
            z_copy(t, k).start()

        @pl.when(is_self(t, k))
        def _():
            zbuf[z] = last[t, part]

    def z_wait(source):
        remote(zbuf.at[source], zbuf.at[source], z_send.at[0, 0], z_recv.at[source], partner).wait_recv()

    for dz in range(1, ZS):
        z_wait((z + dz) % ZS)

    @pl.when(core != z // 2)
    def _():
        z_wait(z)

    result = (zbuf[0] + zbuf[1]) + (zbuf[2] + zbuf[3])
    for e in range(EXPERTS):
        out_ref[:, e, :] = result[:, e * FF : (e + 1) * FF]

    for copy in (*tiles, send_x, *send_g):
        copy.wait_send()
    for copy in mirrors.values():
        copy.wait_send()
    for copy in sends:
        copy.wait_send()
    for t in range(2):
        for k in range(2):

            @pl.when(jnp.logical_not(is_self(t, k)))
            def _():
                z_copy(t, k).wait_send()


def update(sum_ref, one_ref, two_ref, grad_ref, first_ref, second_ref, step_ref):
    grad_total = sum_ref[...]
    new_first = beta_one * one_ref[...] + (1.0 - beta_one) * grad_total
    new_second = beta_two * two_ref[...] + (1.0 - beta_two) * grad_total * grad_total
    grad_ref[...] = grad_total
    first_ref[...] = new_first
    second_ref[...] = new_second
    step_ref[...] = new_first / bias_first / (jnp.sqrt(new_second / bias_second) + adam_epsilon)


def per_device(saved_inputs, hidden_grads, block_expert, live_counts, first_moment, second_moment):
    any_spec = pl.BlockSpec(memory_space=pl.ANY)
    smem_spec = pl.BlockSpec(memory_space=pltpu.SMEM)
    summed = pl.pallas_call(
        kernel,
        out_shape=jax.ShapeDtypeStruct((32, EXPERTS, FF), jnp.float32),
        in_specs=[smem_spec, smem_spec, any_spec, any_spec],
        out_specs=pl.BlockSpec(memory_space=pltpu.VMEM),
        scratch_shapes=[
            pltpu.VMEM((2, 2, ROWS, HALF), jnp.bfloat16),
            pltpu.VMEM((2, ROWS, FF), jnp.bfloat16),
            pltpu.VMEM((2, 2, ROWS, WIDE), jnp.bfloat16),
            pltpu.VMEM((YS, 2, 64, WIDE), jnp.float32),
            pltpu.VMEM((YS, 2, 64, WIDE), jnp.bfloat16),
            pltpu.VMEM((YS, 2, 64, WIDE), jnp.bfloat16),
            pltpu.VMEM((4, 2, 64, WIDE), jnp.float32),
            pltpu.VMEM((3, 2, 64, WIDE), jnp.float32),
            pltpu.VMEM((2, 64, WIDE), jnp.float32),
            pltpu.VMEM((ZS, 32, WIDE), jnp.float32),
            pltpu.SemaphoreType.DMA((3,)),
            pltpu.SemaphoreType.DMA((8,)),
            pltpu.SemaphoreType.DMA((8,)),
            pltpu.SemaphoreType.DMA((3,)),
            pltpu.SemaphoreType.DMA((3,)),
            pltpu.SemaphoreType.DMA((8, 4)),
            pltpu.SemaphoreType.DMA((8, 4)),
            pltpu.SemaphoreType.DMA((4, 4)),
            pltpu.SemaphoreType.DMA((4, 4)),
            pltpu.SemaphoreType.DMA((3, 4)),
            pltpu.SemaphoreType.DMA((3, 4)),
            pltpu.SemaphoreType.DMA((2, 2)),
            pltpu.SemaphoreType.DMA((ZS,)),
            pltpu.SemaphoreType.REGULAR,
            pltpu.SemaphoreType.REGULAR((ZS - 1,)),
            pltpu.SemaphoreType.REGULAR((ZS - 1,)),
        ],
        compiler_params=pltpu.CompilerParams(
            collective_id=0, has_side_effects=True, vmem_limit_bytes=66700000
        ),
    )(
        block_expert.reshape(2, NBLK),
        live_counts.reshape(2, EXPERTS),
        saved_inputs.reshape(2, ROWS, D),
        hidden_grads.reshape(2, ROWS, FF),
    )
    outs = pl.pallas_call(
        update,
        out_shape=[jax.ShapeDtypeStruct((32, EXPERTS, FF), jnp.float32)] * 4,
        in_specs=[pl.BlockSpec(memory_space=pltpu.VMEM)] * 3,
        out_specs=[pl.BlockSpec(memory_space=pltpu.VMEM)] * 4,
    )(summed, first_moment[0], second_moment[0])
    return tuple(value[None] for value in outs)


def solution(mesh):
    in_specs = (
        P("section", "dp", None, None, None),
        P("section", "dp", None, None, None),
        P("section", "dp", None, None),
        P("section", "dp", None, None),
        P("section", "dp", None, None),
        P("section", "dp", None, None),
    )
    out_specs = (
        P("section", "dp", None, None),
        P("section", "dp", None, None),
        P("section", "dp", None, None),
        P("section", "dp", None, None),
    )
    return jax.shard_map(
        per_device, mesh=mesh, in_specs=in_specs, out_specs=out_specs, check_vma=False
    )
```
